32 devices in a mesh: src: 8 (over z, x), dst: 4 (over y, core).
Axes of the slice: x: 2, y: 2, z: 4, core: 2. Of those that a mesh axis runs over, the one named last changes fastest.
Arguments:
- src_table: bfloat16 [1024, 400], P(('src', 'dst')), may hold values from -2.5 to 2.5
- dst_table: bfloat16 [768, 400], P(('dst', 'src')), may hold values from -2.5 to 2.5
- rel_diag: float32 [512, 400], replicated, may hold values from 0.1 to 1.9
- src_index: int32 [8, 4, 512], P('src', 'dst'), may hold values from 0 to 127
- dst_index: int32 [8, 4, 512], P('src', 'dst'), may hold values from 0 to 191
- rel_index: int32 [8, 4, 512], P('src', 'dst'), may hold values from 0 to 511
- neg_index: int32 [8, 4, 2, 512], P('src', 'dst'), may hold values from 0 to 191
- edge_count: int32 [8, 4], P('src', 'dst'), may hold values from 32 to 512, as said below
Outputs:
- grad_src: float32 [1024, 400], P(('src', 'dst'))
- grad_dst: float32 [768, 400], P(('dst', 'src'))
- grad_rel: float32 [512, 400], replicated
The draws below stay inside these ranges and needn't reach their ends.
Inputs may be any that keep to these rules, and one draw needn't show every extreme that they name: Edge slots 0 to edge_count[a, b] - 1 of bucket (a, b) are live and the rest are ignored; some bucket has exactly 512 live edges and some has exactly 32.
All inputs are finite; a program needn't handle non-finite values.
Results may differ from the reference program's by a relative error of at most 0.0021.
Values may be sent and summed in bfloat16 or wider, within the bound.
No kernel may reach another device: no remote copies, remote signals or barrier semaphores. Data moves between devices by JAX's collectives and lax.ppermute only.
A program may use at most 64 MiB of HBM per device.

```python
import math
import jax
import jax.numpy as jnp
from jax import lax

D = 400
R = 512
E_CAP = 512
CH = 256
NEG = 512
PROWS_S = 128
PROWS_D = 192
SPANS = 2
N_SRC = 8
N_DST = 4


def draw_edge_count(key, part):
    keys = jax.random.split(jax.random.fold_in(key, 7), 4)
    total = N_SRC * N_DST
    shifts = jax.random.randint(keys[0], (total,), 0, 4)
    divisor = jnp.left_shift(jnp.ones((total,), jnp.int32), shifts)
    base = E_CAP // divisor
    lower = jax.random.randint(keys[1], (total,), 0, E_CAP // 16 + 1)
    counts = base - lower
    top_bucket = jax.random.randint(keys[2], (), 0, total)
    low_bucket = (top_bucket + 1 + jax.random.randint(keys[3], (), 0, total - 1)) % total
    counts = counts.at[top_bucket].set(E_CAP).at[low_bucket].set(E_CAP // 16)
    return counts.reshape(N_SRC, N_DST).astype(jnp.int32)


def place_ends(array, key, smallest, high):
    longest = array.shape.index(max(array.shape))
    spots = []
    for shift in (0, 1):
        where = [jax.random.randint(jax.random.fold_in(key, axis), (), 0, length) for axis, length in enumerate(array.shape)]
        where[longest] = (where[longest] + shift) % array.shape[longest]
        spots.append(tuple(where))
    return array.at[spots[0]].set(smallest).at[spots[1]].set(high)


def steps_of(key, extent, pieces, low, largest):
    level, own = 1.0, jax.random.fold_in(key, 6)
    for axis_at, parts in pieces:
        heights = jnp.exp(jax.random.uniform(jax.random.fold_in(own, axis_at), (parts,), jnp.float32, low / len(pieces), largest / len(pieces)))
        level = level * jnp.repeat(heights, extent[axis_at] // parts).reshape([-1 if axis == axis_at else 1 for axis in range(len(extent))])
    return level


def centred(stream_key, shape, scale, reach, shards=(), kind=jnp.bfloat16):
    gain = steps_of(stream_key, shape, shards, -0.22, 0.18) if shards else 1.0
    array = jax.random.normal(stream_key, shape, jnp.float32) * scale * gain
    return jnp.minimum(jnp.maximum(array, -reach), reach).astype(kind)


def setup_inputs(seed: int = 0) -> dict:
    splits = jax.random.split(jax.random.key(seed), 9)
    src_table = centred(splits[0], (N_SRC * PROWS_S, D), 0.35, 2.5, ((0, 32),))
    dst_table = centred(splits[1], (N_DST * PROWS_D, D), 0.35, 2.5, ((0, 32),))
    rel_diag = jnp.clip(1.0 + 0.18 * jax.random.normal(splits[2], (R, D), jnp.float32), 0.1, 1.9)
    src_index = place_ends(jax.random.randint(splits[3], (N_SRC, N_DST, E_CAP), 0, PROWS_S), jax.random.fold_in(splits[3], 1), 0, PROWS_S - 1).astype(jnp.int32)
    dst_index = place_ends(jax.random.randint(splits[4], (N_SRC, N_DST, E_CAP), 0, PROWS_D), jax.random.fold_in(splits[4], 1), 0, PROWS_D - 1).astype(jnp.int32)
    rel_index = place_ends(jax.random.randint(splits[5], (N_SRC, N_DST, E_CAP), 0, R), jax.random.fold_in(splits[5], 1), 0, R - 1).astype(jnp.int32)
    neg_index = place_ends(jax.random.randint(splits[6], (N_SRC, N_DST, SPANS, NEG), 0, PROWS_D), jax.random.fold_in(splits[6], 1), 0, PROWS_D - 1).astype(jnp.int32)
    edge_count = draw_edge_count(jax.random.fold_in(splits[8], 71), 0)
    return {"src_table": src_table, "dst_table": dst_table, "rel_diag": rel_diag, "src_index": src_index, "dst_index": dst_index, "rel_index": rel_index, "neg_index": neg_index, "edge_count": edge_count}


def bucket_terms(source_part, target_part, rel_diag, source_rows, target_rows, relation_rows, negative_rows, live_count):
    inverse = 1.0 / math.sqrt(NEG)
    live_mask = (jnp.arange(E_CAP, dtype=jnp.int32) < live_count).astype(jnp.float32)
    source_vec = jnp.take(source_part, source_rows, axis=0).astype(jnp.float32)
    target_vec = jnp.take(target_part, target_rows, axis=0).astype(jnp.float32)
    relation_vec = jnp.take(rel_diag, relation_rows, axis=0)
    scaled = source_vec * relation_vec
    rounded = scaled.astype(jnp.bfloat16)
    positive = lax.optimization_barrier(jnp.sum(scaled * target_vec, axis=1))
    weight_pos = -live_mask * jax.nn.sigmoid(-positive)
    negative_vec = jnp.take(target_part, negative_rows.reshape(-1), axis=0).reshape(SPANS, NEG, D).astype(jnp.float32)
    grouped = rounded.reshape(SPANS, CH, D).astype(jnp.float32)
    scores = jnp.einsum('ced,cnd->cen', grouped, negative_vec)
    weight_neg = (live_mask.reshape(SPANS, CH, 1) * jax.nn.sigmoid(scores) * inverse).astype(jnp.bfloat16).astype(jnp.float32)
    pulled = jnp.einsum('cen,cnd->ced', weight_neg, negative_vec).reshape(E_CAP, D)
    pushed = jnp.einsum('cen,ced->cnd', weight_neg, grouped).reshape(SPANS * NEG, D)
    grad_mix = weight_pos[:, None] * target_vec + pulled
    source_grad = jnp.zeros((PROWS_S, D), jnp.float32).at[source_rows].add(relation_vec * grad_mix)
    relation_grad = jnp.zeros((R, D), jnp.float32).at[relation_rows].add(source_vec * grad_mix)
    target_grad = jnp.zeros((PROWS_D, D), jnp.float32).at[target_rows].add(weight_pos[:, None] * scaled)
    target_grad = target_grad.at[negative_rows.reshape(-1)].add(pushed)
    return (source_grad, target_grad, relation_grad)

def reference(src_table, dst_table, rel_diag, src_index, dst_index, rel_index, neg_index, edge_count):

    def visit(carry, bucket):
        grad_source, grad_target, grad_relation = carry
        first = (bucket // N_DST).astype(jnp.int32)
        second = (bucket % N_DST).astype(jnp.int32)
        source_start = (first * PROWS_S).astype(jnp.int32)
        target_start = (second * PROWS_D).astype(jnp.int32)
        source_part = lax.dynamic_slice_in_dim(src_table, source_start, PROWS_S, 0)
        target_part = lax.dynamic_slice_in_dim(dst_table, target_start, PROWS_D, 0)
        source_grad, target_grad, relation_grad = bucket_terms(source_part, target_part, rel_diag, src_index[first, second], dst_index[first, second], rel_index[first, second], neg_index[first, second], edge_count[first, second])
        old_source = lax.dynamic_slice_in_dim(grad_source, source_start, PROWS_S, 0)
        grad_source = lax.dynamic_update_slice_in_dim(grad_source, old_source + source_grad, source_start, 0)
        old_target = lax.dynamic_slice_in_dim(grad_target, target_start, PROWS_D, 0)
        grad_target = lax.dynamic_update_slice_in_dim(grad_target, old_target + target_grad, target_start, 0)
        return ((grad_source, grad_target, grad_relation + relation_grad), None)
    start = (jnp.zeros((N_SRC * PROWS_S, D), jnp.float32), jnp.zeros((N_DST * PROWS_D, D), jnp.float32), jnp.zeros((R, D), jnp.float32))
    result, unused = lax.scan(visit, start, jnp.arange(N_SRC * N_DST, dtype=jnp.int32))
    return (result[0], result[1], result[2])
```

```python
import functools
import math

import jax
import jax.numpy as jnp
from jax import lax
from jax.experimental import pallas as pl
from jax.experimental.pallas import tpu as pltpu
from jax.sharding import PartitionSpec as P

F32, BF16, I32 = jnp.float32, jnp.bfloat16, jnp.int32


def bits_of(n):
    count = n.bit_length() - 1
    assert 1 << count == n
    return count


def reverse(value, count):
    return sum(((value >> k) & 1) << (count - 1 - k) for k in range(count))


def swap(x, axis, n, bit):
    return lax.ppermute(x, axis, [(i, i ^ (1 << bit)) for i in range(n)])


def split(x):
    high = x.astype(BF16)
    return high, (x - high.astype(F32)).astype(BF16)


def dot(a, b):
    return jnp.dot(a, b, preferred_element_type=F32)


def dot_t(a, b):
    return lax.dot_general(a, b, (((1,), (1,)), ((), ())), preferred_element_type=F32)


def labelled_rows(label, own, owners, rows):
    count = bits_of(owners)
    out, before = label, 0
    for o in range(owners):
        shift = ((reverse(o, count) ^ own) - o) * rows
        if o == 0:
            out = out + shift
        else:
            out = out + jnp.where(label >= o * rows, shift - before, 0)
        before = shift
    return out


def one_hot(a, b):
    return jnp.where(a == b, 1.0, 0.0).astype(BF16)


def columns(rows):
    n = rows[0].shape[1]
    stack = jnp.concatenate(rows + [jnp.zeros((8 - len(rows), n), I32)], axis=0)
    turned = stack.T
    return [turned[:, k : k + 1] for k in range(len(rows))]


def relation_kernel(rel_index, rel_diag, out):
    rows = rel_diag.shape[0]
    edges = rel_index.shape[1]
    (column,) = columns([rel_index[...]])
    pick = one_hot(column, lax.broadcasted_iota(I32, (edges, rows), 1))
    high, low = split(rel_diag[...])
    out[...] = dot(pick, high) + dot(pick, low)


def bucket_kernel(
    sizes, edge_count, place, source, target, relation, src_index, dst_index, rel_index, neg_index,
    keep_out, send_out, dst_out,
):
    n_src, n_dst = sizes
    edges, width = relation.shape
    prow_s, prow_d, rels = source.shape[0], target.shape[0], rel_rows(keep_out, source)
    spans, negs = neg_index.shape
    per_span = edges // spans
    inverse = 1.0 / math.sqrt(negs)
    live_count = edge_count[0, 0]
    a, b, mask = place[0], place[1], place[2]
    src_row, dst_row, rel_row = src_index[...], dst_index[...], rel_index[...]
    neg_rows = [neg_index[c : c + 1, :] for c in range(spans)]
    turned = columns([src_row, dst_row] + neg_rows)
    src_col, dst_col, neg_cols = turned[0], turned[1], turned[2:]

    def labels(shape, axis, own, owners):
        return labelled_rows(
            lax.broadcasted_iota(I32, shape, axis), own, owners, shape[axis] // owners
        )

    s_lane = labels((1, prow_s), 1, b, n_dst)
    s_sub = labels((prow_s, 1), 0, b, n_dst)
    d_lane = labels((1, prow_d), 1, a, n_src)
    d_sub = labels((prow_d, 1), 0, a, n_src)
    r_sub = lax.broadcasted_iota(I32, (rels, 1), 0) ^ mask

    part = target[...]
    s = dot(one_hot(src_col, s_lane), source[...])
    t = dot(one_hot(dst_col, d_lane), part)
    r = relation[...]
    q = s * r
    qb = q.astype(BF16)
    live_col = jnp.where(lax.broadcasted_iota(I32, (edges, 1), 0) < live_count, 1.0, 0.0)
    live_lane = jnp.where(lax.broadcasted_iota(I32, (1, edges), 1) < live_count, 1.0, 0.0)
    p = jnp.sum(q * t, axis=1, keepdims=True)
    w = -live_col * jax.nn.sigmoid(-p)

    scores = dot_t(qb, part)
    weights = (live_col * jax.nn.sigmoid(scores) * inverse).astype(BF16).astype(F32)
    scores_t = dot_t(part, qb)
    weights_t = (live_lane * jax.nn.sigmoid(scores_t) * inverse).astype(BF16)
    pulled = []
    pushed = jnp.zeros((prow_d, width), F32)
    for c in range(spans):
        at = slice(c * per_span, (c + 1) * per_span)
        count_lane = jnp.sum(jnp.where(neg_cols[c] == d_lane, 1.0, 0.0), axis=0, keepdims=True)
        count_sub = jnp.sum(jnp.where(neg_rows[c] == d_sub, 1.0, 0.0), axis=1, keepdims=True)
        high, low = split(weights[at] * count_lane)
        pulled.append(dot(high, part) + dot(low, part))
        pushed = pushed + count_sub * dot(weights_t[:, at], qb[at])
    g = w * t + jnp.concatenate(pulled, axis=0)

    def scatter(pick, x):
        high, low = split(x)
        return dot(pick, high) + dot(pick, low)

    rel_half, src_half = rels // 2, prow_s // 2
    rel_grad = scatter(one_hot(rel_row, r_sub), s * g)
    src_grad = scatter(one_hot(src_row, s_sub), r * g)
    keep_out[:rel_half] = rel_grad[:rel_half]
    send_out[:rel_half] = rel_grad[rel_half:]
    keep_out[rel_half:] = src_grad[:src_half]
    send_out[rel_half:] = src_grad[src_half:]
    dst_out[...] = scatter(one_hot(dst_row, d_sub), w * q) + pushed


def rel_rows(keep_out, source):
    return 2 * keep_out.shape[0] - source.shape[0]


def place_kernel(blocks, place, own, other, out):
    mask = place[2]
    half = own.shape[0]
    size = 2 * half // blocks
    for j in range(blocks):
        piece = own if j < blocks // 2 else other
        at = j * size % half
        start = pl.multiple_of((j * size) ^ mask, size)
        out[pl.ds(start, size), :] = piece[at : at + size, :]


VMEM = pl.BlockSpec(memory_space=pltpu.VMEM)
SMEM = pl.BlockSpec(memory_space=pltpu.SMEM)


def per_device(
    n_src, n_dst, src_table, dst_table, rel_diag, src_index, dst_index, rel_index, neg_index, edge_count
):
    width = src_table.shape[1]
    edges = src_index.shape[-1]
    rels = rel_diag.shape[0]
    bits_src, bits_dst = bits_of(n_src), bits_of(n_dst)
    total = bits_src + bits_dst
    blocks = n_src * n_dst
    a, b = lax.axis_index("src"), lax.axis_index("dst")
    order = [("dst", n_dst, k) for k in range(bits_dst)] + [("src", n_src, k) for k in range(bits_src)]
    mine = 0
    for step, (axis, n, k) in enumerate(order):
        bit = ((b if axis == "dst" else a) >> k) & 1
        mine = mine + (bit << (total - 1 - step))
    place = jnp.stack([a, b, mine * (rels // blocks)]).astype(I32)
    src_row, dst_row, rel_row = (x.reshape(1, edges) for x in (src_index, dst_index, rel_index))
    neg_rows = neg_index.reshape(neg_index.shape[2:])

    source, target = src_table, dst_table
    for k in reversed(range(max(bits_src, bits_dst))):
        if k < bits_dst:
            source = jnp.concatenate([source, swap(source, "dst", n_dst, k)], axis=0)
        if k < bits_src:
            target = jnp.concatenate([target, swap(target, "src", n_src, k)], axis=0)
    relation = pl.pallas_call(
        relation_kernel,
        out_shape=jax.ShapeDtypeStruct((edges, width), F32),
        in_specs=[VMEM] * 2,
        out_specs=VMEM,
    )(rel_row, rel_diag)

    prow_s, prow_d = source.shape[0], target.shape[0]
    first = (rels + prow_s) // 2
    keep, send, dst_grad = pl.pallas_call(
        functools.partial(bucket_kernel, (n_src, n_dst)),
        out_shape=[
            jax.ShapeDtypeStruct((first, width), F32),
            jax.ShapeDtypeStruct((first, width), F32),
            jax.ShapeDtypeStruct((prow_d, width), F32),
        ],
        in_specs=[SMEM, SMEM] + [VMEM] * 7,
        out_specs=[VMEM] * 3,
    )(edge_count, place, source, target, relation, src_row, dst_row, rel_row, neg_rows)

    rel, src_grad = keep[: rels // 2], keep[rels // 2 :]
    got = swap(send, "dst", n_dst, 0)
    rel, src_grad = rel + got[: rels // 2], src_grad + got[rels // 2 :]
    for step, (axis, n, k) in enumerate(order):
        if step == 0:
            continue
        narrow = k == (1 if axis == "dst" else 0)
        other = src_grad if axis == "dst" else dst_grad
        r_half, o_half = rel.shape[0] // 2, other.shape[0] // 2
        send = jnp.concatenate([rel[r_half:], other[o_half:]], axis=0)
        if narrow:
            send = send.astype(BF16)
        got = swap(send, axis, n, k).astype(F32)
        rel = rel[:r_half] + got[:r_half]
        other = other[:o_half] + got[r_half:]
        if axis == "dst":
            src_grad = other
        else:
            dst_grad = other
    for axis, n, k in reversed(order[1:]):
        rel = jnp.concatenate([rel, swap(rel, axis, n, k)], axis=0)
    last = swap(rel, "dst", n_dst, 0)
    rel_out = pl.pallas_call(
        functools.partial(place_kernel, blocks),
        out_shape=jax.ShapeDtypeStruct((rels, width), F32),
        in_specs=[SMEM] + [VMEM] * 2,
        out_specs=VMEM,
    )(place, rel, last)
    return (src_grad, dst_grad, rel_out)


def solution(mesh):
    sizes = (mesh.shape["src"], mesh.shape["dst"])
    return jax.shard_map(
        functools.partial(per_device, *sizes),
        mesh=mesh,
        in_specs=(
            P(("src", "dst"), None),
            P(("dst", "src"), None),
            P(),
            P("src", "dst", None),
            P("src", "dst", None),
            P("src", "dst", None),
            P("src", "dst", None, None),
            P("src", "dst"),
        ),
        out_specs=(P(("src", "dst"), None), P(("dst", "src"), None), P()),
        check_vma=False,
    )
```

```python
import functools
import math

import jax
import jax.numpy as jnp
from jax import lax
from jax.experimental import pallas as pl
from jax.experimental.pallas import tpu as pltpu
from jax.sharding import PartitionSpec as P

F32, BF16, I32 = jnp.float32, jnp.bfloat16, jnp.int32
VMEM = pl.BlockSpec(memory_space=pltpu.VMEM)
SMEM = pl.BlockSpec(memory_space=pltpu.SMEM)


def bits_of(n):
    count = n.bit_length() - 1
    assert 1 << count == n
    return count


class Grid:
    def __init__(self, n_src, n_dst):
        self.n_src, self.n_dst = n_src, n_dst
        self.ny = n_dst // 2
        self.x_bits = bits_of(n_src) // 2
        self.nx = 1 << self.x_bits
        self.nz = n_src // self.nx
        self.n_plane = self.ny * self.nx
        bits_of(n_dst)

    def swap(self, x, core=0, y=0, x_=0, z=0):
        mask = ((z * self.nx + x_) * self.ny + y) * 2 + core
        n = self.n_src * self.n_dst
        return lax.ppermute(x, ("src", "dst"), [(i, i ^ mask) for i in range(n)])

    def src_owner(self, o):
        return (o % self.ny) * 2 + o // self.ny

    def dst_owner(self, o):
        return (o % self.nz) * self.nx + o // self.nz


def split(x):
    high = x.astype(BF16)
    return high, (x - high.astype(F32)).astype(BF16)


def dot(a, b):
    return jnp.dot(a, b, preferred_element_type=F32)


def dot_t(a, b):
    return lax.dot_general(a, b, (((1,), (1,)), ((), ())), preferred_element_type=F32)


def labelled_rows(label, own, owner_of, owners, rows):
    out, before = label, 0
    for o in range(owners):
        shift = ((owner_of(o) ^ own) - o) * rows
        if o == 0:
            out = out + shift
        else:
            out = out + jnp.where(label >= o * rows, shift - before, 0)
        before = shift
    return out


def one_hot(a, b):
    return jnp.where(a == b, 1.0, 0.0).astype(BF16)


def columns(rows):
    n = rows[0].shape[1]
    stack = jnp.concatenate(rows + [jnp.zeros((8 - len(rows), n), I32)], axis=0)
    turned = stack.T
    return [turned[:, k : k + 1] for k in range(len(rows))]


def relation_kernel(rel_index, rel_turned, out):
    rows = rel_turned.shape[1]
    edges = rel_index.shape[1]
    (column,) = columns([rel_index[...]])
    pick = one_hot(column, lax.broadcasted_iota(I32, (edges, rows), 1))
    high, low = split(rel_turned[...])
    out[...] = dot_t(pick, high) + dot_t(pick, low)


def bucket_kernel(grid, n_source, n_target, *refs):
    edge_count, place, src_index, dst_index, rel_index, neg_index, relation = refs[:7]
    source = jnp.concatenate([r[...] for r in refs[7 : 7 + n_source]], axis=0)
    part = jnp.concatenate([r[...] for r in refs[7 + n_source : 7 + n_source + n_target]], axis=0)
    keep_out, send_out, dst_out = refs[7 + n_source + n_target :]
    edges, width = relation.shape
    prow_s, prow_d = source.shape[0], part.shape[0]
    rels = 2 * keep_out.shape[0] - prow_s
    spans, negs = neg_index.shape
    per_span = edges // spans
    inverse = 1.0 / math.sqrt(negs)
    live_count = edge_count[0, 0]
    a, b, mask = place[0], place[1], place[2]
    src_row, dst_row, rel_row = src_index[...], dst_index[...], rel_index[...]
    neg_rows = [neg_index[c : c + 1, :] for c in range(spans)]
    turned = columns([src_row, dst_row] + neg_rows)
    src_col, dst_col, neg_cols = turned[0], turned[1], turned[2:]

    def s_labels(shape, axis):
        label = lax.broadcasted_iota(I32, shape, axis)
        return labelled_rows(label, b, grid.src_owner, grid.n_dst, prow_s // grid.n_dst)

    def d_labels(shape, axis):
        label = lax.broadcasted_iota(I32, shape, axis)
        return labelled_rows(label, a, grid.dst_owner, grid.n_src, prow_d // grid.n_src)

    s_lane, s_sub = s_labels((1, prow_s), 1), s_labels((prow_s, 1), 0)
    d_lane, d_sub = d_labels((1, prow_d), 1), d_labels((prow_d, 1), 0)
    r_sub = lax.broadcasted_iota(I32, (rels, 1), 0) ^ mask

    s = dot(one_hot(src_col, s_lane), source)
    t = dot(one_hot(dst_col, d_lane), part)
    r = relation[...]
    q = s * r
    qb = q.astype(BF16)
    live_col = jnp.where(lax.broadcasted_iota(I32, (edges, 1), 0) < live_count, 1.0, 0.0)
    live_lane = jnp.where(lax.broadcasted_iota(I32, (1, edges), 1) < live_count, 1.0, 0.0)
    p = jnp.sum(q * t, axis=1, keepdims=True)
    w = -live_col * jax.nn.sigmoid(-p)

    scores = dot_t(qb, part)
    weights = (live_col * jax.nn.sigmoid(scores) * inverse).astype(BF16).astype(F32)
    scores_t = dot_t(part, qb)
    weights_t = (live_lane * jax.nn.sigmoid(scores_t) * inverse).astype(BF16)
    pulled = []
    pushed = jnp.zeros((prow_d, width), F32)
    for c in range(spans):
        at = slice(c * per_span, (c + 1) * per_span)
        count_lane = jnp.sum(jnp.where(neg_cols[c] == d_lane, 1.0, 0.0), axis=0, keepdims=True)
        count_sub = jnp.sum(jnp.where(neg_rows[c] == d_sub, 1.0, 0.0), axis=1, keepdims=True)
        high, low = split(weights[at] * count_lane)
        pulled.append(dot(high, part) + dot(low, part))
        pushed = pushed + count_sub * dot(weights_t[:, at], qb[at])
    g = w * t + jnp.concatenate(pulled, axis=0)

    def scatter(pick, x):
        high, low = split(x)
        return dot(pick, high) + dot(pick, low)

    rel_half, src_half = rels // 2, prow_s // 2
    rel_grad = scatter(one_hot(rel_row, r_sub), s * g)
    src_grad = scatter(one_hot(src_row, s_sub), r * g)
    keep_out[:rel_half] = rel_grad[:rel_half]
    send_out[:rel_half] = rel_grad[rel_half:]
    keep_out[rel_half:] = src_grad[:src_half]
    send_out[rel_half:] = src_grad[src_half:]
    dst_out[...] = scatter(one_hot(dst_row, d_sub), w * q) + pushed


def plane_masks(grid):
    return [(m >> grid.x_bits, m & (grid.nx - 1)) for m in range(grid.n_plane)]


def core_sum_kernel(grid, rel_half, keep, got, dst, own_rel, own_src, own_dst, *sends):
    block = rel_half // grid.n_plane
    s_block = (keep.shape[0] - rel_half) // grid.ny
    d_block = dst.shape[0] // grid.nx

    def rows(start, size):
        return keep[start : start + size, :] + got[start : start + size, :]

    own_rel[...] = rows(0, block)
    own_src[...] = rows(rel_half, s_block)
    own_dst[...] = dst[:d_block, :]
    for m, (y, x) in enumerate(plane_masks(grid)):
        if m == 0:
            continue
        parts = [rows(m * block, block)]
        if x == 0:
            parts.append(rows(rel_half + y * s_block, s_block))
        if y == 0:
            parts.append(dst[x * d_block : (x + 1) * d_block, :])
        sends[m - 1][...] = jnp.concatenate(parts, axis=0).astype(BF16)


def plane_sum_kernel(grid, own_rel, own_src, own_dst, *refs):
    gots, outs = refs[: grid.n_plane - 1], refs[grid.n_plane - 1 :]
    own_out, src_out, dst_keep, sends = outs[0], outs[1], outs[2], outs[3:]
    block = own_rel.shape[0]
    rel, src, dst = own_rel[...], own_src[...], own_dst[...]
    for m, (y, x) in enumerate(plane_masks(grid)):
        if m == 0:
            continue
        got = gots[m - 1][...].astype(F32)
        rel = rel + got[:block]
        if x == 0:
            src = src + got[block : block + src.shape[0]]
        if y == 0:
            dst = dst + got[block : block + dst.shape[0]]
    d_block = dst.shape[0] // grid.nz
    src_out[...] = src
    dst_keep[...] = dst[:d_block]
    narrow = rel.astype(BF16)
    own_out[...] = narrow
    for k in range(1, grid.nz):
        sends[k - 1][:block] = narrow
        sends[k - 1][block:] = dst[k * d_block : (k + 1) * d_block].astype(BF16)


def tree_sum(parts):
    while len(parts) > 1:
        parts = [parts[i] + parts[i + 1] for i in range(0, len(parts), 2)]
    return parts[0]


def line_sum_kernel(own, dst_keep, *refs):
    gots, (rel_out, dst_out) = refs[:-2], refs[-2:]
    block = own.shape[0]
    rel_out[...] = tree_sum([own[...].astype(F32)] + [g[:block].astype(F32) for g in gots])
    dst = dst_keep[...]
    for g in gots:
        dst = dst + g[block:].astype(F32)
    dst_out[...] = dst


def place_kernel(place, *refs):
    pieces, out, held = refs[:-2], refs[-2], refs[-1]
    size = pieces[0].shape[0]
    for j, piece in enumerate(pieces):
        start = pl.multiple_of((j * size) ^ place[2], size)
        held[pl.ds(start, size), :] = piece[...]
    out[...] = held[...].T


def call(kernel, out_shapes, *args, scalars=0, scratch=()):
    return pl.pallas_call(
        kernel,
        out_shape=out_shapes,
        in_specs=[SMEM] * scalars + [VMEM] * (len(args) - scalars),
        out_specs=jax.tree.map(lambda _: VMEM, out_shapes),
        scratch_shapes=scratch,
        compiler_params=pltpu.CompilerParams(vmem_limit_bytes=28 << 20),
    )(*args)


def per_device(
    grid, src_table, dst_table, rel_diag, src_index, dst_index, rel_index, neg_index, edge_count
):
    width = src_table.shape[1]
    edges = src_index.shape[-1]
    rels = rel_diag.shape[0]
    prow_s, prow_d = src_table.shape[0] * grid.n_dst, dst_table.shape[0] * grid.n_src

    def f32(rows):
        return jax.ShapeDtypeStruct((rows, width), F32)

    def bf16(rows):
        return jax.ShapeDtypeStruct((rows, width), BF16)

    block = rels // (2 * grid.n_plane)
    a, b = lax.axis_index("src"), lax.axis_index("dst")
    mine = ((b & 1) * grid.ny + (b >> 1)) * grid.nx + (a & (grid.nx - 1))
    place = jnp.stack([a, b, mine * block]).astype(I32)
    src_row, dst_row, rel_row = (x.reshape(1, edges) for x in (src_index, dst_index, rel_index))
    neg_rows = neg_index.reshape(neg_index.shape[2:])

    source = jnp.concatenate([src_table] + [grid.swap(src_table, y=y) for y in range(1, grid.ny)])
    target = jnp.concatenate([dst_table] + [grid.swap(dst_table, z=z) for z in range(1, grid.nz)])
    sources = [source, grid.swap(source, core=1)]
    targets = [target] + [grid.swap(target, x_=x) for x in range(1, grid.nx)]
    relation = call(relation_kernel, f32(edges), rel_row, rel_diag.T)

    first = (rels + prow_s) // 2
    keep, send, dst_grad = call(
        functools.partial(bucket_kernel, grid, len(sources), len(targets)),
        [f32(first), f32(first), f32(prow_d)],
        edge_count, place, src_row, dst_row, rel_row, neg_rows, relation, *sources, *targets,
        scalars=2,
    )
    got = grid.swap(send, core=1)

    masks = plane_masks(grid)[1:]
    s_block, d_block = prow_s // grid.n_dst, prow_d // grid.nx
    sizes = [block + s_block * (x == 0) + d_block * (y == 0) for y, x in masks]
    own_rel, own_src, own_dst, *sends = call(
        functools.partial(core_sum_kernel, grid, rels // 2),
        [f32(block), f32(s_block), f32(d_block)] + [bf16(n) for n in sizes],
        keep, got, dst_grad,
    )
    gots = [grid.swap(x, y=m[0], x_=m[1]) for x, m in zip(sends, masks)]
    d_line = d_block // grid.nz
    own, src_out, dst_keep, *sends = call(
        functools.partial(plane_sum_kernel, grid),
        [bf16(block), f32(s_block), f32(d_line)] + [bf16(block + d_line)] * (grid.nz - 1),
        own_rel, own_src, own_dst, *gots,
    )
    gots = [grid.swap(x, z=k + 1) for k, x in enumerate(sends)]
    rel, dst_out = call(line_sum_kernel, [f32(block), f32(d_line)], own, dst_keep, *gots)

    pieces = [rel] + [grid.swap(rel, y=y, x_=x) for y, x in masks]
    pieces += [grid.swap(piece, core=1) for piece in pieces]
    rel_out = call(
        place_kernel,
        jax.ShapeDtypeStruct((width, rels), F32),
        place, *pieces,
        scalars=1, scratch=[pltpu.VMEM((rels, width), F32)],
    )
    return (src_out, dst_out, rel_out.T)


def solution(mesh):
    grid = Grid(mesh.shape["src"], mesh.shape["dst"])
    return jax.shard_map(
        functools.partial(per_device, grid),
        mesh=mesh,
        in_specs=(
            P(("src", "dst"), None),
            P(("dst", "src"), None),
            P(),
            P("src", "dst", None),
            P("src", "dst", None),
            P("src", "dst", None),
            P("src", "dst", None, None),
            P("src", "dst"),
        ),
        out_specs=(P(("src", "dst"), None), P(("dst", "src"), None), P()),
        check_vma=False,
    )
```

```python
import functools
import math

import jax
import jax.numpy as jnp
from jax import lax
from jax.experimental import pallas as pl
from jax.experimental.pallas import tpu as pltpu
from jax.sharding import PartitionSpec as P

F32, BF16, I32 = jnp.float32, jnp.bfloat16, jnp.int32
VMEM = pl.BlockSpec(memory_space=pltpu.VMEM)
LANES = 128
SMEM = pl.BlockSpec(memory_space=pltpu.SMEM)


def bits_of(n):
    count = n.bit_length() - 1
    assert 1 << count == n
    return count


class Grid:
    def __init__(self, n_src, n_dst):
        self.n_src, self.n_dst = n_src, n_dst
        self.ny = n_dst // 2
        self.x_bits = bits_of(n_src) // 2
        self.nx = 1 << self.x_bits
        self.nz = n_src // self.nx
        self.n_plane = self.ny * self.nx
        bits_of(n_dst)

    def swap(self, x, core=0, y=0, x_=0, z=0):
        mask = ((z * self.nx + x_) * self.ny + y) * 2 + core
        n = self.n_src * self.n_dst
        return lax.ppermute(x, ("src", "dst"), [(i, i ^ mask) for i in range(n)])

    def src_owner(self, o):
        return (o % self.ny) * 2 + o // self.ny

    def dst_owner(self, o):
        return (o % self.nz) * self.nx + o // self.nz


def split(x):
    high = x.astype(BF16)
    return high, (x - high.astype(F32)).astype(BF16)


def dot(a, b):
    return jnp.dot(a, b, preferred_element_type=F32)


def dot_t(a, b):
    return lax.dot_general(a, b, (((1,), (1,)), ((), ())), preferred_element_type=F32)


def labelled_rows(label, own, owner_of, owners, rows):
    out, before = label, 0
    for o in range(owners):
        shift = ((owner_of(o) ^ own) - o) * rows
        if o == 0:
            out = out + shift
        else:
            out = out + jnp.where(label >= o * rows, shift - before, 0)
        before = shift
    return out


class Pack:
    def __init__(self, width):
        self.full, self.rest = width // LANES, width % LANES
        assert self.rest and LANES % self.rest == 0
        self.per = LANES // self.rest

    def size(self, rows):
        assert rows % self.per == 0
        n = self.full * rows + rows // self.per
        return -(-n // 8) * 8

    def tails(self, x, held):
        rows, start = x.shape[0], self.full * LANES
        held[:rows, : self.rest] = x[:, start:]
        at = [held[pl.ds(g, rows // self.per, stride=self.per), :] for g in range(self.per)]
        return jnp.concatenate([part[:, : self.rest] for part in at], axis=1)

    def store(self, x, tails, out, start, first, rows):
        for j in range(self.full):
            out[start + j * rows : start + (j + 1) * rows, :] = x[
                first : first + rows, j * LANES : (j + 1) * LANES
            ]
        at, n = start + self.full * rows, rows // self.per
        out[at : at + n, :] = tails[first // self.per : first // self.per + n]

    def load(self, ref, out, tail_held):
        rows = out.shape[0]
        for j in range(self.full):
            out[:, j * LANES : (j + 1) * LANES] = ref[j * rows : (j + 1) * rows, :]
        at, n, start = self.full * rows, rows // self.per, self.full * LANES
        tail = ref[at : at + n, :]
        for g in range(self.per):
            part = tail[:, g * self.rest : (g + 1) * self.rest]
            tail_held[pl.ds(g, n, stride=self.per), : self.rest] = part
        out[:, start:] = tail_held[:rows, : self.rest]


def one_hot(a, b):
    return jnp.where(a == b, 1.0, 0.0).astype(BF16)


def columns(rows):
    n = rows[0].shape[1]
    stack = jnp.concatenate(rows + [jnp.zeros((8 - len(rows), n), I32)], axis=0)
    turned = stack.T
    return [turned[:, k : k + 1] for k in range(len(rows))]


def relation_kernel(rel_index, rel_turned, out):
    rows = rel_turned.shape[1]
    edges = rel_index.shape[1]
    (column,) = columns([rel_index[...]])
    pick = one_hot(column, lax.broadcasted_iota(I32, (edges, rows), 1))
    high, low = split(rel_turned[...])
    out[...] = dot_t(pick, high) + dot_t(pick, low)


def bucket_kernel(grid, pack, n_source, n_target, rels, *refs):
    edge_count, place, src_index, dst_index, rel_index, neg_index, relation = refs[:7]
    source = jnp.concatenate([r[...] for r in refs[7 : 7 + n_source]], axis=0)
    part = jnp.concatenate([r[...] for r in refs[7 + n_source : 7 + n_source + n_target]], axis=0)
    keep_out, send_out, dst_out, held = refs[7 + n_source + n_target :]
    edges, width = relation.shape
    prow_s, prow_d = source.shape[0], part.shape[0]
    spans, negs = neg_index.shape
    per_span = edges // spans
    inverse = 1.0 / math.sqrt(negs)
    live_count = edge_count[0, 0]
    a, b, mask = place[0], place[1], place[2]
    src_row, dst_row, rel_row = src_index[...], dst_index[...], rel_index[...]
    neg_rows = [neg_index[c : c + 1, :] for c in range(spans)]
    turned = columns([src_row, dst_row] + neg_rows)
    src_col, dst_col, neg_cols = turned[0], turned[1], turned[2:]

    def s_labels(shape, axis):
        label = lax.broadcasted_iota(I32, shape, axis)
        return labelled_rows(label, b, grid.src_owner, grid.n_dst, prow_s // grid.n_dst)

    def d_labels(shape, axis):
        label = lax.broadcasted_iota(I32, shape, axis)
        return labelled_rows(label, a, grid.dst_owner, grid.n_src, prow_d // grid.n_src)

    s_lane, s_sub = s_labels((1, prow_s), 1), s_labels((prow_s, 1), 0)
    d_lane, d_sub = d_labels((1, prow_d), 1), d_labels((prow_d, 1), 0)
    r_sub = lax.broadcasted_iota(I32, (rels, 1), 0) ^ mask

    s = dot(one_hot(src_col, s_lane), source)
    t = dot(one_hot(dst_col, d_lane), part)
    r = relation[...]
    q = s * r
    qb = q.astype(BF16)
    live_col = jnp.where(lax.broadcasted_iota(I32, (edges, 1), 0) < live_count, 1.0, 0.0)
    live_lane = jnp.where(lax.broadcasted_iota(I32, (1, edges), 1) < live_count, 1.0, 0.0)
    p = jnp.sum(q * t, axis=1, keepdims=True)
    w = -live_col * jax.nn.sigmoid(-p)

    scores = dot_t(qb, part)
    weights = (live_col * jax.nn.sigmoid(scores) * inverse).astype(BF16).astype(F32)
    scores_t = dot_t(part, qb)
    weights_t = (live_lane * jax.nn.sigmoid(scores_t) * inverse).astype(BF16)
    pulled = []
    pushed = jnp.zeros((prow_d, width), F32)
    for c in range(spans):
        at = slice(c * per_span, (c + 1) * per_span)
        count_lane = jnp.sum(jnp.where(neg_cols[c] == d_lane, 1.0, 0.0), axis=0, keepdims=True)
        count_sub = jnp.sum(jnp.where(neg_rows[c] == d_sub, 1.0, 0.0), axis=1, keepdims=True)
        high, low = split(weights[at] * count_lane)
        pulled.append(dot(high, part) + dot(low, part))
        pushed = pushed + count_sub * dot(weights_t[:, at], qb[at])
    g = w * t + jnp.concatenate(pulled, axis=0)

    def scatter(pick, x):
        high, low = split(x)
        return dot(pick, high) + dot(pick, low)

    rel_grad = scatter(one_hot(rel_row, r_sub), s * g)
    src_grad = scatter(one_hot(src_row, s_sub), r * g)
    dst_grad = scatter(one_hot(dst_row, d_sub), w * q) + pushed
    at = 0
    for x, blocks in ((rel_grad, grid.n_plane), (src_grad, grid.ny)):
        tails = pack.tails(x, held)
        rows = x.shape[0] // (2 * blocks)
        for o in range(2 * blocks):
            out = (keep_out, send_out)[o // blocks]
            pack.store(x, tails, out, at + o % blocks * pack.size(rows), o * rows, rows)
        at += blocks * pack.size(rows)
    tails = pack.tails(dst_grad, held)
    rows = prow_d // grid.n_src
    for o in range(grid.n_src):
        pack.store(dst_grad, tails, dst_out, o * pack.size(rows), o * rows, rows)


def plane_masks(grid):
    return [(m >> grid.x_bits, m & (grid.nx - 1)) for m in range(grid.n_plane)]


def core_sum_kernel(grid, block, s_block, keep, got, dst, own_rel, own_src, own_dst, *sends):
    half = block * grid.n_plane
    d_block = dst.shape[0] // grid.nx

    def rows(start, size):
        return keep[start : start + size, :] + got[start : start + size, :]

    own_rel[...] = rows(0, block)
    own_src[...] = rows(half, s_block)
    own_dst[...] = dst[:d_block, :]
    for m, (y, x) in enumerate(plane_masks(grid)):
        if m == 0:
            continue
        parts = [rows(m * block, block)]
        if x == 0:
            parts.append(rows(half + y * s_block, s_block))
        if y == 0:
            parts.append(dst[x * d_block : (x + 1) * d_block, :])
        sends[m - 1][...] = jnp.concatenate(parts, axis=0).astype(BF16)


def plane_sum_kernel(grid, own_rel, own_dst, *refs):
    gots, outs = refs[: grid.n_plane - 1], refs[grid.n_plane - 1 :]
    own_out, dst_keep, sends = outs[0], outs[1], outs[2:]
    block = own_rel.shape[0]
    rel, dst = own_rel[...], own_dst[...]
    for m, (y, x) in enumerate(plane_masks(grid)):
        if m == 0:
            continue
        got = gots[m - 1][...].astype(F32)
        rel = rel + got[:block]
        if y == 0:
            dst = dst + got[block : block + dst.shape[0]]
    d_block = dst.shape[0] // grid.nz
    dst_keep[...] = dst[:d_block]
    narrow = rel.astype(BF16)
    own_out[...] = narrow
    for k in range(1, grid.nz):
        part = dst[k * d_block : (k + 1) * d_block]
        sends[k - 1][...] = jnp.concatenate([rel, part], axis=0).astype(BF16)


def tree_sum(parts):
    while len(parts) > 1:
        parts = [parts[i] + parts[i + 1] for i in range(0, len(parts), 2)]
    return parts[0]


def line_sum_kernel(own, *refs):
    gots, rel_out = refs[:-1], refs[-1]
    block = own.shape[0]
    rel_out[...] = tree_sum([own[...].astype(F32)] + [g[...].astype(F32)[:block] for g in gots])


def finish_kernel(grid, pack, block, own_src, dst_keep, *refs):
    gots, (src_out, dst_out, src_held, dst_held, tail) = refs[:-5], refs[-5:]
    src, dst = own_src[...], dst_keep[...]
    n_src = grid.ny - 1
    for got in gots[:n_src]:
        src = src + got[...].astype(F32)[block : block + src.shape[0]]
    for got in gots[n_src:]:
        dst = dst + got[...].astype(F32)[block:]
    src_held[...] = src
    dst_held[...] = dst
    pack.load(src_held, src_out, tail)
    pack.load(dst_held, dst_out, tail)


def place_kernel(pack, rows, place, *refs):
    pieces, (out, held, tail) = refs[:-3], refs[-3:]
    size = pieces[0].shape[0]
    for j, piece in enumerate(pieces):
        start = pl.multiple_of((j ^ place[3]) * size, 8)
        held[pl.ds(start, size), :] = piece[...]
    n = len(pieces)
    for j in range(pack.full):
        x = [held[b * size + j * rows : b * size + (j + 1) * rows, :] for b in range(n)]
        out[j * LANES : (j + 1) * LANES, :] = jnp.concatenate(x, axis=0).T
    at, few = pack.full * rows, rows // pack.per
    rest = jnp.concatenate([held[b * size + at : b * size + at + few, :] for b in range(n)], axis=0)
    for g in range(pack.per):
        part = rest[:, g * pack.rest : (g + 1) * pack.rest]
        tail[pl.ds(g, n * few, stride=pack.per), : pack.rest] = part
    out[pack.full * LANES :, :] = tail[...].T[: pack.rest]


def call(kernel, out_shapes, *args, scalars=0, scratch=(), flops=None):
    return pl.pallas_call(
        kernel,
        out_shape=out_shapes,
        in_specs=[SMEM] * scalars + [VMEM] * (len(args) - scalars),
        out_specs=jax.tree.map(lambda _: VMEM, out_shapes),
        scratch_shapes=scratch,
        cost_estimate=flops and pl.CostEstimate(flops=flops, bytes_accessed=2 << 20, transcendentals=0),
        compiler_params=pltpu.CompilerParams(vmem_limit_bytes=28 << 20),
    )(*args)


def per_device(
    grid, src_table, dst_table, rel_diag, src_index, dst_index, rel_index, neg_index, edge_count
):
    width = src_table.shape[1]
    edges = src_index.shape[-1]
    rels = rel_diag.shape[0]
    prow_s, prow_d = src_table.shape[0] * grid.n_dst, dst_table.shape[0] * grid.n_src

    pack = Pack(width)

    def f32(rows, lanes=LANES):
        return jax.ShapeDtypeStruct((rows, lanes), F32)

    def bf16(rows):
        return jax.ShapeDtypeStruct((rows, LANES), BF16)

    block = rels // (2 * grid.n_plane)
    a, b = lax.axis_index("src"), lax.axis_index("dst")
    mine = ((b & 1) * grid.ny + (b >> 1)) * grid.nx + (a & (grid.nx - 1))
    place = jnp.stack([a, b, mine * block, mine]).astype(I32)
    src_row, dst_row, rel_row = (x.reshape(1, edges) for x in (src_index, dst_index, rel_index))
    neg_rows = neg_index.reshape(neg_index.shape[2:])

    source = jnp.concatenate([src_table] + [grid.swap(src_table, y=y) for y in range(1, grid.ny)])
    target = jnp.concatenate([dst_table] + [grid.swap(dst_table, z=z) for z in range(1, grid.nz)])
    sources = [source, grid.swap(source, core=1)]
    targets = [target] + [grid.swap(target, x_=x) for x in range(1, grid.nx)]
    relation = call(
        relation_kernel, f32(edges, width), rel_row, rel_diag.T, flops=4 * edges * rels * width
    )

    p_rel = pack.size(block)
    p_src, p_dst = pack.size(src_table.shape[0]), pack.size(dst_table.shape[0])
    first = grid.n_plane * p_rel + grid.ny * p_src
    keep, send, dst_grad = call(
        functools.partial(bucket_kernel, grid, pack, len(sources), len(targets), rels),
        [f32(first), f32(first), f32(p_dst * grid.n_src)],
        edge_count, place, src_row, dst_row, rel_row, neg_rows, relation, *sources, *targets,
        scalars=2, scratch=[pltpu.VMEM((max(rels, prow_s, prow_d), LANES), F32)],
    )
    got = grid.swap(send, core=1)

    masks = plane_masks(grid)[1:]
    p_line = grid.nz * p_dst
    sizes = [p_rel + p_src * (x == 0) + p_line * (y == 0) for y, x in masks]
    own_rel, own_src, own_dst, *sends = call(
        functools.partial(core_sum_kernel, grid, p_rel, p_src),
        [f32(p_rel), f32(p_src), f32(p_line)] + [bf16(n) for n in sizes],
        keep, got, dst_grad,
    )
    gots = [grid.swap(x, y=m[0], x_=m[1]) for x, m in zip(sends, masks)]
    own, dst_keep, *sends = call(
        functools.partial(plane_sum_kernel, grid),
        [bf16(p_rel), f32(p_dst)] + [bf16(p_rel + p_dst)] * (grid.nz - 1),
        own_rel, own_dst, *gots,
    )
    line = [grid.swap(x, z=k + 1) for k, x in enumerate(sends)]
    rel = call(line_sum_kernel, f32(p_rel), own, *line)
    src_out, dst_out = call(
        functools.partial(finish_kernel, grid, pack, p_rel),
        [f32(prow_s // grid.n_dst, width), f32(prow_d // grid.n_src, width)],
        own_src, dst_keep, *[g for g, m in zip(gots, masks) if m[1] == 0], *line,
        scratch=[pltpu.VMEM((n, LANES), F32) for n in (p_src, p_dst, max(p_src, p_dst))],
    )

    pieces = [rel] + [grid.swap(rel, y=y, x_=x) for y, x in masks]
    pieces += [grid.swap(piece, core=1) for piece in pieces]
    rel_out = call(
        functools.partial(place_kernel, pack, block),
        f32(width, rels),
        place, *pieces,
        scalars=1,
        scratch=[pltpu.VMEM((p_rel * len(pieces), LANES), F32), pltpu.VMEM((rels, LANES), F32)],
    )
    return (src_out, dst_out, rel_out.T)


def solution(mesh):
    grid = Grid(mesh.shape["src"], mesh.shape["dst"])
    return jax.shard_map(
        functools.partial(per_device, grid),
        mesh=mesh,
        in_specs=(
            P(("src", "dst"), None),
            P(("dst", "src"), None),
            P(),
            P("src", "dst", None),
            P("src", "dst", None),
            P("src", "dst", None),
            P("src", "dst", None, None),
            P("src", "dst"),
        ),
        out_specs=(P(("src", "dst"), None), P(("dst", "src"), None), P()),
        check_vma=False,
    )
```
